32 devices in a mesh: groups: 2 (over x), expert: 8 (over z, y), section: 2 (over core).
Axes of the slice: x: 2, y: 2, z: 4, core: 2. Of those that a mesh axis runs over, the one named last changes fastest.
Arguments:
- states: bfloat16 [2, 4096, 2048], P('section', ('groups', 'expert')), parts along dimension 1, may hold values from -6 to 6
- k_cache: bfloat16 [2, 1024, 4, 128], P('section', 'groups'), parts along dimension 1, may hold values from -600 to 600, as said below
- v_cache: bfloat16 [2, 1024, 4, 128], P('section', 'groups'), parts along dimension 1, may hold values from -6 to 6
- cache_len: int32 [2, 2], P('section', 'groups'), parts along dimension 1, may hold values from 256 to 512
- expert_ids: int32 [2, 4096, 2], P('section', ('groups', 'expert')), parts along dimension 1, may hold values from 0 to 3, all different within a row
- attn_gain: bfloat16 [2, 2048], P('section'), may hold values from 0.099609375 to 1.8984375
- moe_gain: bfloat16 [2, 2048], P('section'), may hold values from 0.099609375 to 1.8984375
- w_query: bfloat16 [2, 2048, 2048], P('section', None, 'expert'), may hold values from -0.125 to 0.125
- w_key: bfloat16 [2, 2048, 512], P('section', 'expert'), may hold values from -0.125 to 0.125
- w_value: bfloat16 [2, 2048, 512], P('section', 'expert'), may hold values from -0.125 to 0.125
- w_out: bfloat16 [2, 2048, 2048], P('section', 'expert'), may hold values from -0.125 to 0.125
- w_router: bfloat16 [2, 2048, 4], P('section'), may hold values from -0.5 to 0.5
- w_gate: bfloat16 [2, 8, 2048, 3584], P('section', 'expert'), may hold values from -0.125 to 0.125
- w_up: bfloat16 [2, 8, 2048, 3584], P('section', 'expert'), may hold values from -0.125 to 0.125
- w_down: bfloat16 [2, 8, 3584, 2048], P('section', 'expert'), may hold values from -0.0625 to 0.0625
Outputs:
- next_states: bfloat16 [2, 4096, 2048], P('section', ('groups', 'expert')), parts along dimension 1
The draws below stay inside these ranges and needn't reach their ends.
There are 2 independent parts, one for each index of `groups`. The reference program is written for one: setup_inputs(seed, part) draws one part's arguments, and reference() takes and returns one part's arrays. A program takes and returns all parts, laid end to end along the dimension named above; an argument that names none is the same for every part. Nothing has to cross between parts.
Inputs may be any that keep to these rules, and one draw needn't show every extreme that they name: `expert_ids`: the 2 experts of a token differ. `k_cache`: keys already rotated to their positions.
All inputs are finite; a program needn't handle non-finite values.
Results may differ from the reference program's by a relative error of at most 0.018.
Values may be sent and summed in bfloat16 or wider, within the bound.
A program may use at most 192 MiB of HBM per device.

```python
import math
import jax
import jax.numpy as jnp
from jax import lax

D = 2048
HEADS = 16
HD = 128
KVH = 4
EXPERTS = 4
FF = 7168
TOP = 2
SPAN = 2048
CACHE = 512
ROWS = 256
SPLITS = 2
FF_DEV = 3584
HDEV = 2
CAP = 128
N_EXPERT = 8
N_SECTION = 2


def draw_k_cache(key, part):
    base = jnp.clip(jax.random.normal(key, (N_SECTION, CACHE, KVH, HD), jnp.float32), -6.0, 6.0)
    return base.astype(jnp.bfloat16)


def steps_of(stream_key, dims, cuts, least, largest):
    def one(axis_at, blocks):
        heights = jax.random.uniform(jax.random.fold_in(jax.random.fold_in(stream_key, 6), axis_at), (blocks,), jnp.float32, least / len(cuts), largest / len(cuts))
        return jnp.repeat(jnp.exp(heights), dims[axis_at] // blocks).reshape((-1,) + (1,) * (len(dims) - axis_at - 1))

    loudness = one(*cuts[0])
    for cut in cuts[1:]:
        loudness = loudness * one(*cut)
    return loudness


def picks_of(own_key, rows, number_of, top, lift):
    sequence = jax.random.permutation(jax.random.fold_in(own_key, 1), number_of)
    boost = sequence
    for power in range(3):
        boost = boost * boost // number_of
    boost = boost * lift // number_of
    lots = jax.random.randint(jax.random.fold_in(own_key, 2), (rows, number_of), 0, 4096) + boost
    sure = jax.random.permutation(jax.random.fold_in(own_key, 3), rows)[jnp.arange(number_of) % rows]
    lots = jnp.where(jnp.arange(rows)[:, None] == sure[None, :], 1 << 14, lots)
    score = lots * number_of + jnp.arange(number_of)
    return lax.top_k(score.astype(jnp.int32), top)[1].astype(jnp.int32)


def noise(rng, shape, deviation, reach, cuts=(), kind=jnp.bfloat16):
    drawn = deviation * jax.random.normal(rng, shape, jnp.float32)
    if cuts:
        drawn = drawn * steps_of(rng, shape, cuts, -0.22, 0.18)
    return jnp.clip(drawn, -reach, reach).astype(kind)


def setup_inputs(seed: int = 0, part: int = 0) -> dict:
    splits = jax.random.split(jax.random.key(seed), 16)
    own_keys = jax.random.split(jax.random.fold_in(splits[15], part), 16)
    states = noise(own_keys[0], (N_SECTION, SPAN, D), 1.0, 6.0, ((0, 2), (1, 8)))
    k_cache = draw_k_cache(jax.random.fold_in(jax.random.fold_in(splits[15], part), 71), part)
    v_cache = noise(own_keys[2], (N_SECTION, CACHE, KVH, HD), 1.0, 6.0, ((0, 2),))
    cache_len = jax.random.randint(own_keys[3], (N_SECTION, 1), CACHE // 2, CACHE + 1).astype(jnp.int32)
    expert_ids = picks_of(own_keys[4], N_SECTION * SPAN, EXPERTS, TOP, 8192).reshape((N_SECTION, SPAN, TOP))
    attn_gain = jnp.clip(1.0 + 0.18 * jax.random.normal(splits[5], (N_SECTION, D), jnp.float32), 0.099609375, 1.8984375).astype(jnp.bfloat16)
    moe_gain = jnp.clip(1.0 + 0.18 * jax.random.normal(splits[6], (N_SECTION, D), jnp.float32), 0.099609375, 1.8984375).astype(jnp.bfloat16)
    w_query = noise(splits[7], (N_SECTION, D, HEADS * HD), D ** -0.5, 0.125, ((0, 2), (2, 8)))
    w_key = noise(splits[8], (N_SECTION, D, KVH * HD), D ** -0.5, 0.125, ((0, 2), (1, 8)))
    w_value = noise(splits[9], (N_SECTION, D, KVH * HD), D ** -0.5, 0.125, ((0, 2), (1, 8)))
    w_out = noise(splits[10], (N_SECTION, HEADS * HD, D), (HEADS * HD) ** -0.5, 0.125, ((0, 2), (1, 8)))
    w_router = noise(splits[11], (N_SECTION, D, EXPERTS), (D // 16) ** -0.5, 0.5, ((0, 2),))
    w_gate = noise(splits[12], (N_SECTION, N_EXPERT, D, FF_DEV), D ** -0.5, 0.125, ((0, 2), (1, 8)))
    w_up = noise(splits[13], (N_SECTION, N_EXPERT, D, FF_DEV), D ** -0.5, 0.125, ((0, 2), (1, 8)))
    w_down = noise(splits[14], (N_SECTION, N_EXPERT, FF_DEV, D), FF ** -0.5, 0.0625, ((0, 2), (1, 8)))
    return {"states": states, "k_cache": k_cache, "v_cache": v_cache, "cache_len": cache_len, "expert_ids": expert_ids, "attn_gain": attn_gain, "moe_gain": moe_gain, "w_query": w_query, "w_key": w_key, "w_value": w_value, "w_out": w_out, "w_router": w_router, "w_gate": w_gate, "w_up": w_up, "w_down": w_down}


EPSILON = 1e-05
ROPE_BASE = 1000000.0

def normalize(inputs, gain_vec):
    values = inputs.astype(jnp.float32)
    return values * lax.rsqrt(lax.optimization_barrier(jnp.mean(values * values, axis=-1, keepdims=True)) + EPSILON) * gain_vec.astype(jnp.float32)

def rotate(tensor, positions):
    width_all = tensor.shape[-1]
    half_dim = width_all // 2
    frequency = ROPE_BASE ** (-(jnp.arange(half_dim, dtype=jnp.float32) * 2.0 / width_all))
    angles = positions[:, None] * frequency[None, :]
    cosine = jnp.cos(angles)[:, None, :]
    sine_part = jnp.sin(angles)[:, None, :]
    front_part = tensor[..., :half_dim]
    back_part = tensor[..., half_dim:]
    return jnp.concatenate([front_part * cosine - back_part * sine_part, back_part * cosine + front_part * sine_part], axis=-1)

def route_slots(ids, expert_count, capacity):
    hit_mask = (ids[..., None] == jnp.arange(expert_count, dtype=jnp.int32)).astype(jnp.int32).sum(axis=-2).astype(jnp.int32)
    before = (jnp.cumsum(hit_mask, axis=-2) - hit_mask).astype(jnp.int32)
    slot_pos = jnp.take_along_axis(before, ids, axis=-1).astype(jnp.int32)
    return (slot_pos, slot_pos < capacity)

def expert_piece(rows_in, gate_w, up_w, down_w):
    gate_act = jnp.dot(rows_in, gate_w, preferred_element_type=jnp.float32)
    up_act = jnp.dot(rows_in, up_w, preferred_element_type=jnp.float32)
    hidden = (jax.nn.silu(gate_act) * up_act).astype(jnp.bfloat16)
    return jnp.dot(hidden, down_w, preferred_element_type=jnp.float32).astype(jnp.bfloat16)

def layer(section_idx, states, k_cache, v_cache, cache_len, expert_ids, attn_gain, moe_gain, w_query, w_key, w_value, w_out, w_router, w_gate, w_up, w_down):
    inputs = states[section_idx]
    normed = normalize(inputs, attn_gain[section_idx]).astype(jnp.bfloat16)
    start_at = cache_len[section_idx, 0]
    positions = (start_at + jnp.arange(SPAN, dtype=jnp.int32)).astype(jnp.float32)
    query = jnp.dot(normed, w_query[section_idx], preferred_element_type=jnp.float32).reshape(SPAN, HEADS, HD)
    query = rotate(query, positions).astype(jnp.bfloat16)
    key_new = jnp.dot(normed, w_key[section_idx], preferred_element_type=jnp.float32).reshape(SPAN, KVH, HD)
    key_new = rotate(key_new, positions).astype(jnp.bfloat16)
    value_new = jnp.dot(normed, w_value[section_idx], preferred_element_type=jnp.float32).reshape(SPAN, KVH, HD).astype(jnp.bfloat16)
    all_keys = jnp.concatenate([k_cache[section_idx], key_new], axis=0)
    all_values = jnp.concatenate([v_cache[section_idx], value_new], axis=0)
    key_pos = jnp.arange(CACHE + SPAN, dtype=jnp.int32)
    query_pos = jnp.arange(SPAN, dtype=jnp.int32)
    is_valid = jnp.where(key_pos[None, :] < CACHE, (key_pos < start_at)[None, :], key_pos[None, :] - CACHE <= query_pos[:, None])
    scale_by = 1.0 / math.sqrt(HD)

    def one_head(head_idx):
        shared = head_idx // (HEADS // KVH)
        query_head = lax.dynamic_index_in_dim(query, head_idx, 1, keepdims=False)
        key_head = lax.dynamic_index_in_dim(all_keys, shared, 1, keepdims=False)
        value_head = lax.dynamic_index_in_dim(all_values, shared, 1, keepdims=False)
        scores = jnp.dot(query_head, key_head.T, preferred_element_type=jnp.float32) * scale_by
        scores = jnp.where(is_valid, scores, -jnp.inf)
        top_score = lax.optimization_barrier(jnp.max(scores, axis=-1, keepdims=True))
        exp_scores = jnp.exp(scores - top_score)
        attn_probs = (exp_scores / lax.optimization_barrier(jnp.sum(exp_scores, axis=-1, keepdims=True))).astype(jnp.bfloat16)
        return jnp.dot(attn_probs, value_head, preferred_element_type=jnp.float32).astype(jnp.bfloat16)
    attended = lax.map(one_head, jnp.arange(HEADS, dtype=jnp.int32))
    grouped = attended.reshape(N_EXPERT, HDEV, SPAN, HD).transpose(0, 2, 1, 3).reshape(N_EXPERT, SPAN, HDEV * HD)
    out_groups = w_out[section_idx].reshape(N_EXPERT, HDEV * HD, D)

    def add_group(total, pair):
        term_part = jnp.dot(pair[0], pair[1], preferred_element_type=jnp.float32).astype(jnp.bfloat16)
        term_part = lax.optimization_barrier(term_part)
        return (total + term_part.astype(jnp.float32), None)
    attn_sum, unused = lax.scan(add_group, jnp.zeros((SPAN, D), jnp.float32), (grouped, out_groups))
    mixed = inputs.astype(jnp.float32) + attn_sum
    moe_in = normalize(mixed, moe_gain[section_idx]).astype(jnp.bfloat16)
    ids = expert_ids[section_idx]
    slot_pos, is_kept = route_slots(ids.reshape(N_EXPERT, ROWS, TOP), EXPERTS, CAP)
    slot_pos = slot_pos.reshape(SPAN, TOP)
    is_kept = is_kept.reshape(SPAN, TOP)
    block_idx = (jnp.arange(SPAN, dtype=jnp.int32) // ROWS)[:, None]
    target = jnp.where(is_kept, (block_idx * EXPERTS + ids) * CAP + slot_pos, N_EXPERT * EXPERTS * CAP).astype(jnp.int32)
    buffer = jnp.zeros((N_EXPERT * EXPERTS * CAP, D), jnp.bfloat16)
    buffer = buffer.at[target.reshape(-1)].set(jnp.repeat(moe_in, TOP, axis=0), mode='drop')
    buffer = buffer.reshape(N_EXPERT, EXPERTS, CAP, D)

    def one_piece(device):
        owner = device // SPLITS
        rows_in = lax.dynamic_index_in_dim(buffer, owner, 1, keepdims=False).reshape(N_EXPERT * CAP, D)
        return expert_piece(rows_in, lax.dynamic_index_in_dim(w_gate[section_idx], device, 0, keepdims=False), lax.dynamic_index_in_dim(w_up[section_idx], device, 0, keepdims=False), lax.dynamic_index_in_dim(w_down[section_idx], device, 0, keepdims=False))
    pieces = lax.map(one_piece, jnp.arange(N_EXPERT, dtype=jnp.int32))
    pieces = lax.optimization_barrier(pieces)
    results = pieces.astype(jnp.float32).reshape(EXPERTS, SPLITS, N_EXPERT * CAP, D).sum(axis=1).reshape(EXPERTS * N_EXPERT * CAP, D)
    results = jnp.concatenate([results, jnp.zeros((1, D), jnp.float32)], axis=0)
    where_from = jnp.where(is_kept, ids * (N_EXPERT * CAP) + block_idx * CAP + slot_pos, EXPERTS * N_EXPERT * CAP).astype(jnp.int32)
    logits = jnp.dot(moe_in, w_router[section_idx], preferred_element_type=jnp.float32)
    picked = jnp.take_along_axis(logits, ids, axis=1)
    gate_mix = jnp.stack([jax.nn.sigmoid(picked[:, 0] - picked[:, 1]), jax.nn.sigmoid(picked[:, 1] - picked[:, 0])], axis=1)
    moe_out = lax.optimization_barrier(jnp.sum(gate_mix[:, :, None] * results[where_from], axis=1))
    return (mixed + moe_out).astype(jnp.bfloat16)

def reference(states, k_cache, v_cache, cache_len, expert_ids, attn_gain, moe_gain, w_query, w_key, w_value, w_out, w_router, w_gate, w_up, w_down):
    finished = []
    for section_idx in range(N_SECTION):
        finished.append(layer(section_idx, states, k_cache, v_cache, cache_len, expert_ids, attn_gain, moe_gain, w_query, w_key, w_value, w_out, w_router, w_gate, w_up, w_down))
    return jnp.roll(jnp.stack(finished, axis=0), 1, axis=0)
```

```python
import math

import jax
import jax.numpy as jnp
from jax import lax
from jax.sharding import PartitionSpec as P

EPSILON = 1e-05
ROPE_BASE = 1000000.0


def shifted(shard, axis, by):
    size = lax.axis_size(axis)
    return lax.ppermute(shard, axis, [(i, (i + by) % size) for i in range(size)])


def normalize(inputs, gain_vec):
    values = inputs.astype(jnp.float32)
    return (
        values
        * lax.rsqrt(jnp.mean(values * values, axis=-1, keepdims=True) + EPSILON)
        * gain_vec.astype(jnp.float32)
    )


def body(
    states,
    k_cache,
    v_cache,
    cache_len,
    expert_ids,
    attn_gain,
    moe_gain,
    w_query,
    w_key,
    w_value,
    w_out,
    w_router,
    w_gate,
    w_up,
    w_down,
):
    bf16, f32 = jnp.bfloat16, jnp.float32
    me = lax.axis_index("expert")
    n = lax.axis_size("expert")
    x_rows = states[0]
    rows, width = x_rows.shape
    cache_size, kv_heads, hd = k_cache.shape[1:]
    qw = w_query.shape[2]
    expert_count = w_router.shape[2]
    cols = kv_heads
    m = n // cols
    assert m * cols == n and expert_count == cols
    c, half = me // m, me % m
    heads = m * qw // hd

    def turn(a, by):
        pairs = [(m * i + q, m * i + (q + by) % m) for i in range(cols) for q in range(m)]
        return lax.ppermute(a, "expert", pairs)

    def ring(a, by):
        pairs = [(m * i + q, m * ((i + by) % cols) + q) for i in range(cols) for q in range(m)]
        return lax.ppermute(a, "expert", pairs)

    def line(a, senders, by):
        pairs = [(m * i + q, m * (i + by) + q) for i in senders for q in range(m)]
        return lax.ppermute(a, "expert", pairs)

    def pick(table, index, among):
        out = table[among[0]]
        for j in among[1:]:
            out = jnp.where(index == j, table[j], out)
        return out

    own = normalize(x_rows, attn_gain[0]).astype(bf16)
    wq_parts = [w_query[0]] + [turn(w_query[0], r) for r in range(1, m)]
    kv_own = jnp.concatenate(
        [w_key[0].reshape(-1, kv_heads, hd), w_value[0].reshape(-1, kv_heads, hd)], axis=2
    ).transpose(1, 0, 2)
    kv_rows = kv_own.shape[1]
    gathered = jnp.zeros((cols, kv_rows, 2 * hd), bf16)
    for d in range(cols):
        part = lax.dynamic_index_in_dim(kv_own, (c + d) % cols, 0)
        if d:
            part = ring(part, d)
        gathered = lax.dynamic_update_slice(gathered, part, ((c - d) % cols, 0, 0))
    kv_w = jnp.zeros((cols, m, kv_rows, 2 * hd), bf16)
    for r in range(m):
        part = turn(gathered, r) if r else gathered
        kv_w = lax.dynamic_update_slice(kv_w, part[:, None], (0, (half - r) % m, 0, 0))
    wo = jnp.concatenate([w_out[0]] + [turn(w_out[0], r) for r in range(1, m)], axis=0)
    w_all = jnp.concatenate(wq_parts + [kv_w.reshape(width, 2 * hd)], axis=1)

    start_at = cache_len[0, 0]
    half_dim = hd // 2
    frequency = ROPE_BASE ** (-(jnp.arange(half_dim, dtype=f32) * 2.0 / hd))
    blocks = m * jnp.arange(cols + 1, dtype=jnp.int32) + half
    positions = start_at + blocks[:, None] * rows + jnp.arange(rows, dtype=jnp.int32)
    angles = positions.astype(f32)[:, :, None] * frequency
    cosine, sine = jnp.cos(angles), jnp.sin(angles)

    q_buf = jnp.zeros((cols + 1, rows, m * qw), bf16)
    kv_buf = jnp.zeros((m * (cols + 1), rows, 2 * hd), bf16)

    def project(chunk, col, bufs):
        q_buf, kv_buf = bufs
        mapped = jnp.dot(chunk, w_all, preferred_element_type=f32)
        cos = lax.dynamic_index_in_dim(cosine, col, 0, keepdims=False)[:, None, :]
        sin = lax.dynamic_index_in_dim(sine, col, 0, keepdims=False)[:, None, :]
        turned = mapped[:, : m * qw + hd].reshape(rows, heads + 1, hd)
        a, b = turned[..., :half_dim], turned[..., half_dim:]
        turned = jnp.concatenate([a * cos - b * sin, b * cos + a * sin], axis=-1)
        turned = turned.astype(bf16).reshape(rows, m * qw + hd)
        kv = jnp.concatenate([turned[:, m * qw :], mapped[:, m * qw + hd :].astype(bf16)], axis=1)
        q_buf = lax.dynamic_update_slice(q_buf, turned[None, :, : m * qw], (col, 0, 0))
        for r in range(m):
            part = turn(kv, r) if r else kv
            at = m * col + (half - r) % m
            kv_buf = lax.dynamic_update_slice(kv_buf, part[None], (at, 0, 0))
        return q_buf, kv_buf

    bufs = project(own, c, (q_buf, kv_buf))
    up, down = own, own
    for s in range(1, cols):
        up = line(up, range(s - 1, cols - 1), 1)
        down = line(down, range(1, cols - s + 1), -1)
        if 2 * s < cols:
            bufs = project(up, jnp.where(c >= s, c - s, cols), bufs)
            bufs = project(down, jnp.where(c + s < cols, c + s, cols), bufs)
        else:
            col = jnp.where(c >= s, c - s, jnp.where(c + s < cols, c + s, cols))
            bufs = project(jnp.where(c >= s, up, down), col, bufs)
    q_buf, kv_buf = bufs
    head_slice = lambda cache: lax.dynamic_index_in_dim(cache[0], c, 1, keepdims=False)
    kv_new = kv_buf[: m * cols].reshape(m * cols * rows, 2 * hd)
    all_keys = jnp.concatenate([head_slice(k_cache), kv_new[:, :hd]], axis=0)
    all_values = jnp.concatenate([head_slice(v_cache), kv_new[:, hd:]], axis=0)
    scale_by = 1.0 / math.sqrt(hd)

    def attend(j):
        stop_at = cache_size + m * (j + 1) * rows
        query = q_buf[j].reshape(rows, heads, hd)
        scores = (
            jnp.einsum("qhd,kd->hqk", query, all_keys[:stop_at], preferred_element_type=f32)
            * scale_by
        )
        key_pos = jnp.arange(stop_at, dtype=jnp.int32)
        query_pos = (m * j + half) * rows + jnp.arange(rows, dtype=jnp.int32)
        is_valid = jnp.where(
            key_pos[None, :] < cache_size,
            (key_pos < start_at)[None, :],
            key_pos[None, :] - cache_size <= query_pos[:, None],
        )
        scores = jnp.where(is_valid[None], scores, -jnp.inf)
        top_score = jnp.max(scores, axis=-1, keepdims=True)
        exp_scores = jnp.exp(scores - top_score)
        probs = (exp_scores / jnp.sum(exp_scores, axis=-1, keepdims=True)).astype(bf16)
        out = jnp.einsum("hqk,kd->qhd", probs, all_values[:stop_at], preferred_element_type=f32)
        out = out.astype(bf16).reshape(rows, m * qw)
        return jnp.dot(out, wo, preferred_element_type=f32).astype(bf16)

    parts = {j: attend(j) for j in range(cols)}
    going_up = going_down = None
    for t in range(1, cols):
        far = cols - t
        send_up = pick(parts, c + far, list(range(far, cols)))
        send_down = pick(parts, c - far, list(range(0, t)))
        if going_up is not None:
            send_up = (send_up.astype(f32) + going_up.astype(f32)).astype(bf16)
            send_down = (send_down.astype(f32) + going_down.astype(f32)).astype(bf16)
        going_up = line(send_up, range(0, t), 1)
        going_down = line(send_down, range(far, cols), -1)
    mine = pick(parts, c, list(range(cols)))
    attn_rows = mine.astype(f32) + going_up.astype(f32) + going_down.astype(f32)
    h_rows = x_rows.astype(f32) + attn_rows
    moe_rows = normalize(h_rows, moe_gain[0]).astype(bf16)

    top_k = expert_ids.shape[2]
    cap = rows * top_k // expert_count
    ids = expert_ids[0]
    every = jnp.arange(expert_count, dtype=jnp.int32)
    hits = (ids[:, :, None] == every).astype(jnp.int32)
    hit_any = hits.sum(axis=1)
    before = jnp.cumsum(hit_any, axis=0) - hit_any
    slot = jnp.sum(hits * before[:, None, :], axis=2)
    kept = slot < cap
    logits = jnp.dot(moe_rows, w_router[0], preferred_element_type=f32)
    chosen = jnp.sum(jnp.where(hits > 0, logits[:, None, :], 0.0), axis=2)
    gates = jnp.stack(
        [jax.nn.sigmoid(chosen[:, 0] - chosen[:, 1]), jax.nn.sigmoid(chosen[:, 1] - chosen[:, 0])],
        axis=1,
    )

    def chosen_slots(e):
        named = (ids == e) & kept
        at = jnp.sum(jnp.where(named, slot + 1, 0), axis=1) - 1
        gate = jnp.sum(jnp.where(named, gates, 0.0), axis=1)
        return (at[:, None] == jnp.arange(cap, dtype=jnp.int32)).astype(bf16), gate

    order = sorted(range(cols), key=lambda d: (d > 0, -min(d, cols - d)))
    sent, picks = {}, {}
    for d in order:
        picks[d] = chosen_slots((c + d) % cols)
        packed = jnp.einsum(
            "rs,rd->sd", picks[d][0], moe_rows, preferred_element_type=f32
        ).astype(bf16)
        sent[d] = ring(packed, d) if d else packed

    moe_out = jnp.zeros((rows, width), f32)
    for d in order:
        batch = jnp.concatenate([sent[d]] + [turn(sent[d], r) for r in range(1, m)], axis=0)
        gate_act = jnp.dot(batch, w_gate[0, 0], preferred_element_type=f32)
        up_act = jnp.dot(batch, w_up[0, 0], preferred_element_type=f32)
        hidden = (jax.nn.silu(gate_act) * up_act).astype(bf16)
        result = jnp.dot(hidden, w_down[0, 0], preferred_element_type=f32).astype(bf16)
        summed = result[:cap].astype(f32)
        for r in range(1, m):
            summed = summed + turn(result[r * cap : (r + 1) * cap], -r).astype(f32)
        if d:
            summed = ring(summed.astype(bf16), -d)
        onehot, gate = picks[d]
        spread = jnp.dot(onehot, summed.astype(bf16), preferred_element_type=f32)
        moe_out = moe_out + gate[:, None] * spread
    layer_rows = (h_rows + moe_out).astype(bf16)
    passed = shifted(layer_rows, "section", 1)
    return passed[None]


def solution(mesh):
    in_specs = (
        P("section", ("groups", "expert"), None),
        P("section", "groups", None, None),
        P("section", "groups", None, None),
        P("section", "groups"),
        P("section", ("groups", "expert"), None),
        P("section", None),
        P("section", None),
        P("section", None, "expert"),
        P("section", "expert", None),
        P("section", "expert", None),
        P("section", "expert", None),
        P("section", None, None),
        P("section", "expert", None, None),
        P("section", "expert", None, None),
        P("section", "expert", None, None),
    )
    out_specs = P("section", ("groups", "expert"), None)
    return jax.shard_map(body, mesh=mesh, in_specs=in_specs, out_specs=out_specs, check_vma=False)
```

```python
import math

import jax
import jax.numpy as jnp
from jax import lax
from jax.sharding import PartitionSpec as P


EPSILON = 1e-05
ROPE_BASE = 1000000.0


def shifted(shard, axis, by):
    size = lax.axis_size(axis)
    return lax.ppermute(shard, axis, [(i, (i + by) % size) for i in range(size)])


def normalize(inputs, gain_vec):
    values = inputs.astype(jnp.float32)
    return (
        values
        * lax.rsqrt(jnp.mean(values * values, axis=-1, keepdims=True) + EPSILON)
        * gain_vec.astype(jnp.float32)
    )


def section_step(
    states,
    k_cache,
    v_cache,
    cache_len,
    expert_ids,
    attn_gain,
    moe_gain,
    w_query,
    w_key,
    w_value,
    w_out,
    w_router,
    w_gate,
    w_up,
    w_down,
):
    bf16, f32 = jnp.bfloat16, jnp.float32
    me = lax.axis_index("expert")
    n = lax.axis_size("expert")
    x_rows = states[0]
    rows, width = x_rows.shape
    cache_size, kv_heads, hd = k_cache.shape[1:]
    qw = w_query.shape[2]
    expert_count = w_router.shape[2]
    cols = kv_heads
    m = n // cols
    assert m * cols == n and expert_count == cols
    c, half = me // m, me % m
    heads = m * qw // hd

    def turn(a, by):
        pairs = [(m * i + q, m * i + (q + by) % m) for i in range(cols) for q in range(m)]
        return lax.ppermute(a, "expert", pairs)

    def ring(a, by):
        pairs = [(m * i + q, m * ((i + by) % cols) + q) for i in range(cols) for q in range(m)]
        return lax.ppermute(a, "expert", pairs)

    def line(a, senders, by):
        pairs = [(m * i + q, m * (i + by) + q) for i in senders for q in range(m)]
        return lax.ppermute(a, "expert", pairs)

    def pick(table, index, among):
        out = table[among[0]]
        for j in among[1:]:
            out = jnp.where(index == j, table[j], out)
        return out

    own = normalize(x_rows, attn_gain[0]).astype(bf16)
    wq_parts = [w_query[0]] + [turn(w_query[0], r) for r in range(1, m)]
    kv_own = jnp.concatenate(
        [w_key[0].reshape(-1, kv_heads, hd), w_value[0].reshape(-1, kv_heads, hd)], axis=2
    ).transpose(1, 0, 2)
    kv_rows = kv_own.shape[1]
    gathered = jnp.zeros((cols, kv_rows, 2 * hd), bf16)
    for d in range(cols):
        part = lax.dynamic_index_in_dim(kv_own, (c + d) % cols, 0)
        if d:
            part = ring(part, d)
        gathered = lax.dynamic_update_slice(gathered, part, ((c - d) % cols, 0, 0))
    kv_w = jnp.zeros((cols, m, kv_rows, 2 * hd), bf16)
    for r in range(m):
        part = turn(gathered, r) if r else gathered
        kv_w = lax.dynamic_update_slice(kv_w, part[:, None], (0, (half - r) % m, 0, 0))
    wo = jnp.concatenate([w_out[0]] + [turn(w_out[0], r) for r in range(1, m)], axis=0)
    w_all = jnp.concatenate(wq_parts + [kv_w.reshape(width, 2 * hd)], axis=1)

    start_at = cache_len[0, 0]
    half_dim = hd // 2
    frequency = ROPE_BASE ** (-(jnp.arange(half_dim, dtype=f32) * 2.0 / hd))
    blocks = m * jnp.arange(cols + 1, dtype=jnp.int32) + half
    positions = start_at + blocks[:, None] * rows + jnp.arange(rows, dtype=jnp.int32)
    angles = positions.astype(f32)[:, :, None] * frequency
    cosine, sine = jnp.cos(angles), jnp.sin(angles)

    q_buf = jnp.zeros((cols + 1, rows, m * qw), bf16)
    kv_buf = jnp.zeros((m * (cols + 1), rows, 2 * hd), bf16)

    def project(chunk, col, bufs):
        q_buf, kv_buf = bufs
        mapped = jnp.dot(chunk, w_all, preferred_element_type=f32)
        cos = lax.dynamic_index_in_dim(cosine, col, 0, keepdims=False)[:, None, :]
        sin = lax.dynamic_index_in_dim(sine, col, 0, keepdims=False)[:, None, :]
        turned = mapped[:, : m * qw + hd].reshape(rows, heads + 1, hd)
        a, b = turned[..., :half_dim], turned[..., half_dim:]
        turned = jnp.concatenate([a * cos - b * sin, b * cos + a * sin], axis=-1)
        turned = turned.astype(bf16).reshape(rows, m * qw + hd)
        kv = jnp.concatenate([turned[:, m * qw :], mapped[:, m * qw + hd :].astype(bf16)], axis=1)
        q_buf = lax.dynamic_update_slice(q_buf, turned[None, :, : m * qw], (col, 0, 0))
        for r in range(m):
            part = turn(kv, r) if r else kv
            at = m * col + (half - r) % m
            kv_buf = lax.dynamic_update_slice(kv_buf, part[None], (at, 0, 0))
        return q_buf, kv_buf

    bufs = project(own, c, (q_buf, kv_buf))
    up, down = own, own
    for s in range(1, cols):
        up = line(up, range(s - 1, cols - 1), 1)
        down = line(down, range(1, cols - s + 1), -1)
        if 2 * s < cols:
            bufs = project(up, jnp.where(c >= s, c - s, cols), bufs)
            bufs = project(down, jnp.where(c + s < cols, c + s, cols), bufs)
        else:
            col = jnp.where(c >= s, c - s, jnp.where(c + s < cols, c + s, cols))
            bufs = project(jnp.where(c >= s, up, down), col, bufs)
    q_buf, kv_buf = bufs
    head_slice = lambda cache: lax.dynamic_index_in_dim(cache[0], c, 1, keepdims=False)
    kv_new = kv_buf[: m * cols].reshape(m * cols * rows, 2 * hd)
    all_keys = jnp.concatenate([head_slice(k_cache), kv_new[:, :hd]], axis=0)
    all_values = jnp.concatenate([head_slice(v_cache), kv_new[:, hd:]], axis=0)
    scale_by = 1.0 / math.sqrt(hd)

    def attend(j):
        stop_at = cache_size + m * (j + 1) * rows
        query = q_buf[j].reshape(rows, heads, hd)
        scores = (
            jnp.einsum("qhd,kd->hqk", query, all_keys[:stop_at], preferred_element_type=f32)
            * scale_by
        )
        key_pos = jnp.arange(stop_at, dtype=jnp.int32)
        query_pos = (m * j + half) * rows + jnp.arange(rows, dtype=jnp.int32)
        is_valid = jnp.where(
            key_pos[None, :] < cache_size,
            (key_pos < start_at)[None, :],
            key_pos[None, :] - cache_size <= query_pos[:, None],
        )
        scores = jnp.where(is_valid[None], scores, -jnp.inf)
        top_score = jnp.max(scores, axis=-1, keepdims=True)
        exp_scores = jnp.exp(scores - top_score)
        probs = (exp_scores / jnp.sum(exp_scores, axis=-1, keepdims=True)).astype(bf16)
        out = jnp.einsum("hqk,kd->qhd", probs, all_values[:stop_at], preferred_element_type=f32)
        out = out.astype(bf16).reshape(rows, m * qw)
        return jnp.dot(out, wo, preferred_element_type=f32).astype(bf16)

    parts = {j: attend(j) for j in range(cols)}
    going_up = going_down = None
    for t in range(1, cols):
        far = cols - t
        send_up = pick(parts, c + far, list(range(far, cols)))
        send_down = pick(parts, c - far, list(range(0, t)))
        if going_up is not None:
            send_up = (send_up.astype(f32) + going_up.astype(f32)).astype(bf16)
            send_down = (send_down.astype(f32) + going_down.astype(f32)).astype(bf16)
        going_up = line(send_up, range(0, t), 1)
        going_down = line(send_down, range(far, cols), -1)
    mine = pick(parts, c, list(range(cols)))
    attn_rows = mine.astype(f32) + going_up.astype(f32) + going_down.astype(f32)
    h_rows = x_rows.astype(f32) + attn_rows
    moe_rows = normalize(h_rows, moe_gain[0]).astype(bf16)

    top_k = expert_ids.shape[2]
    cap = rows * top_k // expert_count
    ids = expert_ids[0]
    every = jnp.arange(expert_count, dtype=jnp.int32)
    hits = (ids[:, :, None] == every).astype(jnp.int32)
    hit_any = hits.sum(axis=1)
    before = jnp.cumsum(hit_any, axis=0) - hit_any
    slot = jnp.sum(hits * before[:, None, :], axis=2)
    kept = slot < cap
    logits = jnp.dot(moe_rows, w_router[0], preferred_element_type=f32)
    chosen = jnp.sum(jnp.where(hits > 0, logits[:, None, :], 0.0), axis=2)
    gates = jnp.stack(
        [jax.nn.sigmoid(chosen[:, 0] - chosen[:, 1]), jax.nn.sigmoid(chosen[:, 1] - chosen[:, 0])],
        axis=1,
    )

    def chosen_slots(e):
        named = (ids == e) & kept
        at = jnp.sum(jnp.where(named, slot + 1, 0), axis=1) - 1
        gate = jnp.sum(jnp.where(named, gates, 0.0), axis=1)
        return (at[:, None] == jnp.arange(cap, dtype=jnp.int32)).astype(bf16), gate

    batches = (tuple(range(cols // 2)), tuple(range(cols // 2, cols)))
    sent, picks = {}, {}
    for d in [d for batch in batches for d in batch]:
        picks[d] = chosen_slots((c + d) % cols)
        packed = jnp.einsum(
            "rs,rd->sd", picks[d][0], moe_rows, preferred_element_type=f32
        ).astype(bf16)
        sent[d] = ring(packed, d) if d else packed

    moe_out = jnp.zeros((rows, width), f32)
    for batch in batches:
        pieces = []
        for d in batch:
            pieces.append(sent[d])
            pieces += [turn(sent[d], r) for r in range(1, m)]
        gathered_rows = jnp.concatenate(pieces, axis=0)
        gate_act = jnp.dot(gathered_rows, w_gate[0, 0], preferred_element_type=f32)
        up_act = jnp.dot(gathered_rows, w_up[0, 0], preferred_element_type=f32)
        hidden = (jax.nn.silu(gate_act) * up_act).astype(bf16)
        result = jnp.dot(hidden, w_down[0, 0], preferred_element_type=f32).astype(bf16)
        for at, d in reversed(list(enumerate(batch))):
            base = at * m * cap
            summed = result[base : base + cap].astype(f32)
            for r in range(1, m):
                piece = result[base + r * cap : base + (r + 1) * cap]
                summed = summed + turn(piece, -r).astype(f32)
            summed = summed.astype(bf16)
            if d:
                summed = ring(summed, -d)
            onehot, gate = picks[d]
            spread = jnp.dot(onehot, summed, preferred_element_type=f32)
            moe_out = moe_out + gate[:, None] * spread
    layer_rows = (h_rows + moe_out).astype(bf16)
    passed = shifted(layer_rows, "section", 1)
    return passed[None]


def solution(mesh):
    in_specs = (
        P("section", ("groups", "expert"), None),
        P("section", "groups", None, None),
        P("section", "groups", None, None),
        P("section", "groups"),
        P("section", ("groups", "expert"), None),
        P("section", None),
        P("section", None),
        P("section", None, "expert"),
        P("section", "expert", None),
        P("section", "expert", None),
        P("section", "expert", None),
        P("section", None, None),
        P("section", "expert", None, None),
        P("section", "expert", None, None),
        P("section", "expert", None, None),
    )
    out_specs = P("section", ("groups", "expert"), None)
    return jax.shard_map(section_step, mesh=mesh, in_specs=in_specs, out_specs=out_specs, check_vma=False)
```
